32 devices in a mesh: groups: 2 (over y), seq: 16 (over z, x, core).
Axes of the slice: x: 2, y: 2, z: 4, core: 2. Of those that a mesh axis runs over, the one named last changes fastest.
Arguments:
- queries: bfloat16 [8192, 2048], P(('groups', 'seq')), parts along dimension 0, may hold values from -6 to 6
- keys: bfloat16 [8192, 2048], P(('groups', 'seq')), parts along dimension 0, may hold values from -0.5390625 to 0.5390625
- values: bfloat16 [8192, 2048], P(('groups', 'seq')), parts along dimension 0, may hold values from -6 to 6
- prompt_state: bfloat16 [16, 2048, 128], P('groups', 'seq'), parts along dimension 0, may hold values from -12 to 12
- lengths: int32 [16], P('groups'), parts along dimension 0, may hold values from 1 to 16, 32 in all
- prompt_of: int32 [16, 1], P('groups'), parts along dimension 0, may hold values from 0 to 7
Outputs:
- mixed: bfloat16 [8192, 2048], P(('groups', 'seq')), parts along dimension 0
The draws below stay inside these ranges and needn't reach their ends.
There are 2 independent parts, one for each index of `groups`. The reference program is written for one: setup_inputs(seed, part) draws one part's arguments, and reference() takes and returns one part's arrays. A program takes and returns all parts, laid end to end along the dimension named above; each array names one. Nothing has to cross between parts.
Inputs may be any that keep to these rules, and one draw needn't show every extreme that they name: `lengths`: responses fill the group's blocks exactly in order; the longest has exactly 16 blocks. `prompt_of`: every prompt has exactly one response.
All inputs are finite; a program needn't handle non-finite values.
Results may differ from the reference program's by a relative error of at most 0.0046.
Values may be sent and summed in bfloat16 or wider, within the bound.
A program may use at most 64 MiB of HBM per device.

```python
import math
import jax
import jax.numpy as jnp
import numpy as np
from jax import lax

H = 16
DK = 128
DV = 128
SPAN = 128
PROMPTS = 8
TOKENS = 4096
RESP = 8
MOST = 16


def block_scale(rng, shape, shards, smallest, top_value):
    level, own = 1.0, jax.random.fold_in(rng, 6)
    for axis_at, parts in shards:
        draws = jnp.exp(jax.random.uniform(jax.random.fold_in(own, axis_at), (parts,), jnp.float32, smallest / len(shards), top_value / len(shards)))
        level = level * jnp.repeat(draws, shape[axis_at] // parts).reshape([-1 if axis == axis_at else 1 for axis in range(len(shape))])
    return level


def different_ones(stream_key, rows, number_of, top, lift):
    sequence = jax.random.permutation(jax.random.fold_in(stream_key, 1), number_of)
    boost = sequence
    for power in range(3):
        boost = boost * boost // number_of
    boost = boost * lift // number_of
    lots = jax.random.randint(jax.random.fold_in(stream_key, 2), (rows, number_of), 0, 4096) + boost
    sure = jax.random.permutation(jax.random.fold_in(stream_key, 3), rows)[jnp.arange(number_of) % rows]
    lots = jnp.where(jnp.arange(rows)[:, None] == sure[None, :], 1 << 14, lots)
    priority = lots * number_of + jnp.arange(number_of)
    return lax.top_k(priority.astype(jnp.int32), top)[1].astype(jnp.int32)


def profile(number_of, total, limit, skew):
    portions = [(1 << 20) // math.isqrt(rank ** skew) + 1 for rank in range(2, number_of + 1)]
    surplus, holding = total - limit - (number_of - 1), [1] * (number_of - 1)
    while surplus > 0:
        movable = [i for i in range(number_of - 1) if holding[i] < limit]
        whole, remaining = sum([portions[i] for i in movable]), surplus
        for i in movable:
            extra = min(limit - holding[i], max(1, remaining * portions[i] // whole), surplus)
            holding[i] = holding[i] + extra
            surplus = surplus - extra
    return np.array([limit] + holding)


def uneven_parts(rng, amount, total, limit, lean):
    if amount == 2:
        one = jax.random.randint(rng, (), max(1, total - limit), min(limit, total - 1) + 1)
        return jnp.stack([one, total - one])
    tallies = jnp.asarray(profile(amount, total, limit, lean), jnp.int32)
    pairs = (amount - 1) // 2
    giver, taker = tallies[1:1 + 2 * pairs:2], tallies[2:2 + 2 * pairs:2]
    margin = jnp.minimum(giver - 1, limit - taker)
    moved = jax.random.randint(jax.random.fold_in(rng, 1), (pairs,), 0, 1 << 20) % (margin + 1)
    tallies = tallies.at[1:1 + 2 * pairs:2].set(giver - moved).at[2:2 + 2 * pairs:2].set(taker + moved)
    return tallies[jax.random.permutation(jax.random.fold_in(rng, 2), amount)]


def scatter_about(own_key, extent, scale, most, shards=(), kind=jnp.bfloat16):
    factor_of = block_scale(own_key, extent, shards, -0.22, 0.18) if shards else 1.0
    array = jax.random.normal(own_key, extent, jnp.float32) * scale * factor_of
    return jnp.minimum(jnp.maximum(array, -most), most).astype(kind)


def setup_inputs(seed: int = 0, part: int = 0) -> dict:
    key_of = jax.random.split(jax.random.key(seed), 7)
    own_keys = jax.random.split(jax.random.fold_in(key_of[6], part), 7)
    return {
        "queries": scatter_about(own_keys[0], (TOKENS, H * DK), 1.0, 6.0, ((0, 16),)),
        "keys": scatter_about(own_keys[1], (TOKENS, H * DK), 0.09, 0.5390625, ((0, 16),)),
        "values": scatter_about(own_keys[2], (TOKENS, H * DV), 1.0, 6.0, ((0, 16),)),
        "prompt_state": scatter_about(own_keys[3], (PROMPTS, H * DK, DV), 2.0, 12.0, ((1, 16),)),
        "lengths": uneven_parts(own_keys[4], RESP, TOKENS // SPAN, MOST, 2).astype(jnp.int32),
        "prompt_of": different_ones(own_keys[5], RESP, PROMPTS, 1, 0),
    }


epsilon = 1e-06

def normalize(mixed):
    scale = lax.rsqrt(lax.optimization_barrier(jnp.mean(mixed * mixed, axis=-1, keepdims=True)) + epsilon)
    return mixed * scale

def reference(queries, keys, values, prompt_state, lengths, prompt_of):
    blocks = TOKENS // SPAN
    starts = (jnp.cumsum(lengths) - lengths).astype(jnp.int32)
    block_ids = jnp.arange(blocks, dtype=jnp.int32)
    hits = (starts[None, :] == block_ids[:, None]).astype(jnp.int32)
    is_start = lax.optimization_barrier(jnp.sum(hits, axis=1)) > 0
    block_prompt = lax.optimization_barrier(jnp.sum(hits * prompt_of[:, 0][None, :], axis=1)).astype(jnp.int32)
    query_blocks = queries.reshape(blocks, SPAN, H, DK)
    key_blocks = keys.reshape(blocks, SPAN, H, DK)
    value_blocks = values.reshape(blocks, SPAN, H, DV)
    causal = jnp.tril(jnp.ones((SPAN, SPAN), dtype=bool))
    highest = lax.Precision.HIGHEST

    def advance(carried, inputs):
        query_part, key_part, value_part, starting, which = inputs
        cached = lax.dynamic_index_in_dim(prompt_state, which, 0, keepdims=False)
        cached = cached.astype(jnp.float32).reshape(H, DK, DV)
        state = jnp.where(starting, cached, carried)
        query_wide = query_part.astype(jnp.float32)
        key_wide = key_part.astype(jnp.float32)
        value_wide = value_part.astype(jnp.float32)
        rounded = lax.optimization_barrier(state.astype(jnp.bfloat16)).astype(jnp.float32)
        inter = jnp.einsum('thd,hde->the', query_wide, rounded, precision=highest)
        scores = jnp.einsum('thd,shd->hts', query_wide, key_wide, precision=highest)
        masked = jnp.where(causal[None], scores, jnp.float32(0.0))
        weights = lax.optimization_barrier(masked.astype(jnp.bfloat16)).astype(jnp.float32)
        intra = jnp.einsum('hts,she->the', weights, value_wide, precision=highest)
        mixed = normalize(inter + intra).astype(jnp.bfloat16).reshape(SPAN, H * DV)
        updated = state + jnp.einsum('thd,the->hde', key_wide, value_wide, precision=highest)
        return (updated, mixed)
    initial = jnp.zeros((H, DK, DV), dtype=jnp.float32)
    _, outputs = lax.scan(advance, initial, (query_blocks, key_blocks, value_blocks, is_start, block_prompt))
    return outputs.reshape(TOKENS, H * DV)
```

```python
import functools
import jax
import jax.numpy as jnp
from jax import lax
from jax.experimental import pallas as pl
from jax.experimental.pallas import tpu as pltpu
from jax.sharding import PartitionSpec as P

DK = 128
DV = 128
SPAN = 128
epsilon = 1e-06


def matmul(a, b, ca, cb):
    return lax.dot_general(a, b, (((ca,), (cb,)), ((), ())), preferred_element_type=jnp.float32)


def kernel(n, q_hbm, k_hbm, v_hbm, p_hbm, len_ref, of_ref, out_hbm,
           q_ref, k_ref, v_ref, p_ref, out_ref, intra, first, sum_out, sum_in, st_out, st_in, pr_out, pr_in,
           index, flag, load_sem, out_sem, sum_send, sum_recv, st_send, st_recv, pr_send, pr_recv):
    me = lax.axis_index("seq")
    width = k_ref.shape[1]
    heads = width // DK
    rows = width // n
    pieces = DK // rows
    responses = len_ref.shape[0]

    def load(i, src, dst):
        return pltpu.make_async_copy(src, dst, load_sem.at[i])

    loads = [load(0, p_hbm, p_ref), load(1, k_hbm, k_ref), load(2, v_hbm, v_ref), load(3, q_hbm, q_ref)]
    for copy in loads:
        copy.start()

    barrier = pltpu.get_barrier_semaphore()

    @pl.loop(1, n)
    def _(j):
        pl.semaphore_signal(barrier, inc=1, device_id={"seq": lax.rem(me + j, n)}, device_id_type=pl.DeviceIdType.MESH)

    @pl.loop(0, 2 * n)
    def _(c):
        start = jnp.int32(0)
        begins = jnp.int32(0)
        which = jnp.int32(0)
        for r in range(responses):
            hit = jnp.where(start == c, 1, 0)
            begins = begins + hit
            which = which + hit * of_ref[r, 0]
            start = start + len_ref[r]
        flag[c] = begins
        index[c] = which

    pl.semaphore_wait(barrier, n - 1)

    def send(src, dst, send_sem, recv_sem, target):
        return pltpu.make_async_remote_copy(
            src_ref=src, dst_ref=dst, send_sem=send_sem, recv_sem=recv_sem,
            device_id={"seq": target}, device_id_type=pl.DeviceIdType.MESH)

    loads[0].wait()

    @pl.loop(1, n + 1)
    def _(j):
        target = lax.rem(me + j, n)
        pr_out[target] = p_ref[index[2 * target + 1]]

        @pl.when(target != me)
        def _():
            send(pr_out.at[target], pr_in.at[me], pr_send, pr_recv, target).start()

    pr_in[me] = pr_out[me]

    loads[1].wait()
    loads[2].wait()
    second_starts = flag[2 * me + 1] > 0
    my_head = me // pieces

    @pl.loop(0, heads)
    def _(i):
        h = lax.rem(my_head + 1 + i, heads)
        cols = pl.ds(pl.multiple_of(h * DK, DK), DK)
        a = matmul(k_ref[0:SPAN, cols], v_ref[0:SPAN, cols], 0, 0)
        b = matmul(k_ref[SPAN:2 * SPAN, cols], v_ref[SPAN:2 * SPAN, cols], 0, 0)
        first[h] = a
        total = jnp.where(second_starts, b, a + b).astype(jnp.bfloat16)
        for j in range(pieces):
            owner = h * pieces + j
            sum_out[owner] = total[j * rows:(j + 1) * rows]

            @pl.when(owner != me)
            def _():
                send(sum_out.at[owner], sum_in.at[me], sum_send, sum_recv.at[me], owner).start()

    sum_in[me] = sum_out[me]

    loads[3].wait()
    causal = lax.broadcasted_iota(jnp.int32, (SPAN, SPAN), 0) >= lax.broadcasted_iota(jnp.int32, (SPAN, SPAN), 1)

    @pl.loop(0, heads)
    def _(h):
        cols = pl.ds(pl.multiple_of(h * DK, DK), DK)
        for block in range(2):
            rng = slice(block * SPAN, (block + 1) * SPAN)
            scores = matmul(q_ref[rng, cols], k_ref[rng, cols], 1, 1)
            weights = jnp.where(causal, scores, 0.0).astype(jnp.bfloat16)
            intra[rng, cols] = matmul(weights, v_ref[rng, cols], 1, 0)

    def scan(d, state):
        state = jnp.where(flag[2 * d] > 0, p_ref[index[2 * d]].astype(jnp.float32), state)
        st_out[d] = state.astype(jnp.bfloat16)

        @pl.when(d != me)
        def _():
            send(st_out.at[d], st_in.at[me], st_send, st_recv.at[me], d).start()
            send(sum_out.at[d], sum_in.at[d], sum_send, sum_recv.at[d], d).wait_recv()

        base = jnp.where(flag[2 * d + 1] > 0, p_ref[index[2 * d + 1]].astype(jnp.float32), state)
        return base + sum_in[d].astype(jnp.float32)

    lax.fori_loop(0, n, scan, jnp.zeros((rows, DV), jnp.float32))
    st_in[me] = st_out[me]

    def others(ref):
        return ref.at[0:n - 1]

    pltpu.make_async_copy(others(pr_in), others(pr_in), pr_recv).wait()

    @pl.loop(0, heads)
    def _(h):
        cols = pl.ds(pl.multiple_of(h * DK, DK), DK)
        for j in range(pieces):
            owner = h * pieces + j

            @pl.when(owner != me)
            def _():
                send(st_out.at[owner], st_in.at[owner], st_send, st_recv.at[owner], owner).wait_recv()

        entering = st_in[pl.ds(h * pieces, pieces)].reshape(DK, DV)
        prompt = pr_in[pl.ds(h * pieces, pieces)].reshape(DK, DV)
        later = (entering.astype(jnp.float32) + first[h]).astype(jnp.bfloat16)
        states = (entering, jnp.where(second_starts, prompt, later))
        for block in range(2):
            rng = slice(block * SPAN, (block + 1) * SPAN)
            o = matmul(q_ref[rng, cols], states[block], 1, 0) + intra[rng, cols]
            scale = lax.rsqrt(jnp.mean(o * o, axis=-1, keepdims=True) + epsilon)
            out_ref[rng, cols] = (o * scale).astype(jnp.bfloat16)
        pltpu.make_async_copy(out_ref.at[:, cols], out_hbm.at[:, cols], out_sem).start()

    pltpu.make_async_copy(out_ref, out_hbm, out_sem).wait()
    pltpu.make_async_copy(others(pr_out), others(pr_out), pr_send).wait()
    pltpu.make_async_copy(others(sum_out), others(sum_out), sum_send).wait()
    pltpu.make_async_copy(others(st_out), others(st_out), st_send).wait()


def solution(mesh):
    n = mesh.shape["seq"]

    def shards(queries, keys, values, prompt_state, lengths, prompt_of):
        tokens, width = queries.shape
        prompts, rows, _ = prompt_state.shape
        half = jnp.bfloat16
        anywhere = pl.BlockSpec(memory_space=pl.ANY)
        scalar = pl.BlockSpec(memory_space=pltpu.SMEM)
        piece = pltpu.VMEM((n, rows, DV), half)
        dma = pltpu.SemaphoreType.DMA
        return pl.pallas_call(
            functools.partial(kernel, n),
            out_shape=jax.ShapeDtypeStruct((tokens, width), half),
            in_specs=[anywhere] * 4 + [scalar] * 2,
            out_specs=anywhere,
            scratch_shapes=[
                pltpu.VMEM((tokens, width), half),
                pltpu.VMEM((tokens, width), half),
                pltpu.VMEM((tokens, width), half),
                pltpu.VMEM((prompts, rows, DV), half),
                pltpu.VMEM((tokens, width), half),
                pltpu.VMEM((tokens, width), jnp.float32),
                pltpu.VMEM((width // DK, DK, DV), jnp.float32),
                piece, piece, piece, piece, piece, piece,
                pltpu.SMEM((2 * n,), jnp.int32),
                pltpu.SMEM((2 * n,), jnp.int32),
                dma((4,)), dma(()),
                dma(()), dma((n,)), dma(()), dma((n,)), dma(()), dma(()),
            ],
            compiler_params=pltpu.CompilerParams(
                collective_id=0, has_side_effects=True, vmem_limit_bytes=62 << 20),
        )(queries, keys, values, prompt_state, lengths, prompt_of)

    placed = (
        P(("groups", "seq"), None),
        P(("groups", "seq"), None),
        P(("groups", "seq"), None),
        P("groups", "seq", None),
        P("groups"),
        P("groups", None),
    )
    return jax.shard_map(
        shards, mesh=mesh, in_specs=placed, out_specs=P(("groups", "seq"), None), check_vma=False
    )
```

```python
import functools
import jax
import jax.numpy as jnp
from jax import lax
from jax.experimental import pallas as pl
from jax.experimental.pallas import tpu as pltpu
from jax.sharding import PartitionSpec as P

DK = 128
DV = 128
SPAN = 128
epsilon = 1e-06


def matmul(a, b, ca, cb):
    return lax.dot_general(a, b, (((ca,), (cb,)), ((), ())), preferred_element_type=jnp.float32)


def kernel(n, q_hbm, k_hbm, v_hbm, p_hbm, len_ref, of_ref, out_hbm,
           q_ref, k_ref, v_ref, own_prompts, far_prompts, out_ref, intra, first, sum_out, sum_in, st_out, st_in, pr_out, pr_in,
           over_out, over_in, index, flag, load_sem, out_sem, swap_sem, over_sem, sum_send, sum_recv, st_send, st_recv,
           pr_send, pr_recv):
    me = lax.axis_index("seq")
    half = n // 2
    side = me // half
    own = lax.rem(me, half)
    base = side * half
    partner = lax.rem(me + half, n)
    width = k_ref.shape[1]
    heads = width // DK
    rows = width // n
    pieces = DK // rows
    responses = len_ref.shape[0]

    def load(i, src, dst):
        return pltpu.make_async_copy(src, dst, load_sem.at[i])

    loads = [load(0, p_hbm, own_prompts), load(1, k_hbm, k_ref), load(2, v_hbm, v_ref), load(3, q_hbm, q_ref)]
    for copy in loads:
        copy.start()

    barrier = pltpu.get_barrier_semaphore()

    def greet(device):
        pl.semaphore_signal(barrier, inc=1, device_id={"seq": device}, device_id_type=pl.DeviceIdType.MESH)

    greet(partner)

    @pl.loop(1, half)
    def _(j):
        greet(base + lax.rem(own + j, half))

    @pl.loop(0, n)
    def _(i):
        c = 2 * base + i
        start = jnp.int32(0)
        begins = jnp.int32(0)
        which = jnp.int32(0)
        for r in range(responses):
            hit = jnp.where(start == c, 1, 0)
            begins = begins + hit
            which = which + hit * of_ref[r]
            start = start + len_ref[r]
        flag[i] = begins
        index[i] = which

    pl.semaphore_wait(barrier, half)

    def send(src, dst, send_sem, recv_sem, target):
        return pltpu.make_async_remote_copy(
            src_ref=src, dst_ref=dst, send_sem=send_sem, recv_sem=recv_sem,
            device_id={"seq": target}, device_id_type=pl.DeviceIdType.MESH)

    loads[0].wait()
    swap = send(own_prompts, far_prompts, swap_sem.at[0], swap_sem.at[1], partner)
    swap.start()

    def give_prompts(slot, prompts):
        @pl.loop(1, half + 1)
        def _(j):
            target = lax.rem(own + j, half)
            pr_out[target, slot] = prompts[index[2 * target + 1]]

            @pl.when(target != own)
            def _():
                send(pr_out.at[target, slot], pr_in.at[own, slot], pr_send, pr_recv, base + target).start()

        pr_in[own, slot] = pr_out[own, slot]

    give_prompts(0, own_prompts)

    loads[1].wait()
    loads[2].wait()
    second_starts = flag[2 * own + 1] > 0

    @pl.loop(0, heads // 2)
    def _(i):
        pair = lax.rem(own // pieces + 1 + i, heads // 2)
        for slot in range(2):
            h = pair + lax.rem(side + slot, 2) * (heads // 2)
            cols = pl.ds(pl.multiple_of(h * DK, DK), DK)
            a = matmul(k_ref[0:SPAN, cols], v_ref[0:SPAN, cols], 0, 0)
            b = matmul(k_ref[SPAN:2 * SPAN, cols], v_ref[SPAN:2 * SPAN, cols], 0, 0)
            first[h] = a
            total = jnp.where(second_starts, b, a + b).astype(jnp.bfloat16)
            for j in range(pieces):
                sum_out[pair * pieces + j, slot] = total[j * rows:(j + 1) * rows]
        for j in range(pieces):
            owner = pair * pieces + j

            @pl.when(owner != own)
            def _():
                send(sum_out.at[owner], sum_in.at[own], sum_send, sum_recv.at[own], base + owner).start()

    sum_in[own] = sum_out[own]

    loads[3].wait()
    causal = lax.broadcasted_iota(jnp.int32, (SPAN, SPAN), 0) >= lax.broadcasted_iota(jnp.int32, (SPAN, SPAN), 1)

    @pl.loop(0, heads)
    def _(h):
        cols = pl.ds(pl.multiple_of(h * DK, DK), DK)
        for block in range(2):
            rng = slice(block * SPAN, (block + 1) * SPAN)
            scores = matmul(q_ref[rng, cols], k_ref[rng, cols], 1, 1)
            weights = jnp.where(causal, scores, 0.0).astype(jnp.bfloat16)
            intra[rng, cols] = matmul(weights, v_ref[rng, cols], 1, 0)

    swap.wait_recv()
    give_prompts(1, far_prompts)

    over = send(over_out, over_in, over_sem.at[0], over_sem.at[1], partner)

    @pl.when(side == 0)
    def _():
        over_in[...] = jnp.zeros_like(over_in)

    @pl.when(side == 1)
    def _():
        over.wait_recv()

    def cached(block):
        which = index[block]
        return jnp.stack([own_prompts[which], far_prompts[which]]).astype(jnp.float32)

    def scan(d, state):
        state = jnp.where(flag[2 * d] > 0, cached(2 * d), state)
        st_out[d] = state.astype(jnp.bfloat16)

        @pl.when(d != own)
        def _():
            send(st_out.at[d], st_in.at[own], st_send, st_recv.at[own], base + d).start()
            send(sum_out.at[d], sum_in.at[d], sum_send, sum_recv.at[d], base + d).wait_recv()

        from_here = jnp.where(flag[2 * d + 1] > 0, cached(2 * d + 1), state)
        return from_here + sum_in[d].astype(jnp.float32)

    last = lax.fori_loop(0, half, scan, over_in[...].astype(jnp.float32))

    @pl.when(side == 0)
    def _():
        over_out[0] = last[1].astype(jnp.bfloat16)
        over_out[1] = last[0].astype(jnp.bfloat16)
        over.start()

    st_in[own] = st_out[own]

    def others(ref):
        return ref.at[0:half - 1]

    pltpu.make_async_copy(others(pr_in), others(pr_in), pr_recv).wait()

    @pl.loop(0, heads // 2)
    def _(pair):
        for j in range(pieces):
            owner = pair * pieces + j

            @pl.when(owner != own)
            def _():
                send(st_out.at[owner], st_in.at[owner], st_send, st_recv.at[owner], base + owner).wait_recv()

        for slot in range(2):
            h = pair + lax.rem(side + slot, 2) * (heads // 2)
            cols = pl.ds(pl.multiple_of(h * DK, DK), DK)
            entering = st_in[pl.ds(pair * pieces, pieces), slot].reshape(DK, DV)
            prompt = pr_in[pl.ds(pair * pieces, pieces), slot].reshape(DK, DV)
            later = (entering.astype(jnp.float32) + first[h]).astype(jnp.bfloat16)
            states = (entering, jnp.where(second_starts, prompt, later))
            for block in range(2):
                rng = slice(block * SPAN, (block + 1) * SPAN)
                o = matmul(q_ref[rng, cols], states[block], 1, 0) + intra[rng, cols]
                scale = lax.rsqrt(jnp.mean(o * o, axis=-1, keepdims=True) + epsilon)
                out_ref[rng, cols] = (o * scale).astype(jnp.bfloat16)
            pltpu.make_async_copy(out_ref.at[:, cols], out_hbm.at[:, cols], out_sem).start()

    pltpu.make_async_copy(out_ref, out_hbm, out_sem).wait()
    swap.wait_send()
    pltpu.make_async_copy(others(pr_out), others(pr_out), pr_send).wait()
    pltpu.make_async_copy(others(sum_out), others(sum_out), sum_send).wait()
    pltpu.make_async_copy(others(st_out), others(st_out), st_send).wait()

    @pl.when(side == 0)
    def _():
        over.wait_send()


def solution(mesh):
    n = mesh.shape["seq"]

    def shards(queries, keys, values, prompt_state, lengths, prompt_of):
        tokens, width = queries.shape
        prompts, rows, _ = prompt_state.shape
        half = jnp.bfloat16
        anywhere = pl.BlockSpec(memory_space=pl.ANY)
        scalar = pl.BlockSpec(memory_space=pltpu.SMEM)
        piece = pltpu.VMEM((n // 2, 2, rows, DV), half)
        dma = pltpu.SemaphoreType.DMA
        return pl.pallas_call(
            functools.partial(kernel, n),
            out_shape=jax.ShapeDtypeStruct((tokens, width), half),
            in_specs=[anywhere] * 4 + [scalar] * 2,
            out_specs=anywhere,
            scratch_shapes=[
                pltpu.VMEM((tokens, width), half),
                pltpu.VMEM((tokens, width), half),
                pltpu.VMEM((tokens, width), half),
                pltpu.VMEM((prompts, rows, DV), half),
                pltpu.VMEM((prompts, rows, DV), half),
                pltpu.VMEM((tokens, width), half),
                pltpu.VMEM((tokens, width), jnp.float32),
                pltpu.VMEM((width // DK, DK, DV), jnp.float32),
                piece, piece, piece, piece, piece, piece,
                pltpu.VMEM((2, rows, DV), half),
                pltpu.VMEM((2, rows, DV), half),
                pltpu.SMEM((n,), jnp.int32),
                pltpu.SMEM((n,), jnp.int32),
                dma((4,)), dma(()), dma((2,)), dma((2,)),
                dma(()), dma((n // 2,)), dma(()), dma((n // 2,)), dma(()), dma(()),
            ],
            compiler_params=pltpu.CompilerParams(
                collective_id=0, has_side_effects=True, vmem_limit_bytes=62 << 20),
        )(queries, keys, values, prompt_state, lengths, prompt_of.reshape(-1))

    placed = (
        P(("groups", "seq"), None),
        P(("groups", "seq"), None),
        P(("groups", "seq"), None),
        P("groups", "seq", None),
        P("groups"),
        P("groups", None),
    )
    return jax.shard_map(
        shards, mesh=mesh, in_specs=placed, out_specs=P(("groups", "seq"), None), check_vma=False
    )
```

```python
import functools
import jax
import jax.numpy as jnp
from jax import lax
from jax.experimental import pallas as pl
from jax.experimental.pallas import tpu as pltpu
from jax.sharding import PartitionSpec as P

DK = 128
DV = 128
SPAN = 128
epsilon = 1e-06


def matmul(a, b, ca, cb):
    return lax.dot_general(a, b, (((ca,), (cb,)), ((), ())), preferred_element_type=jnp.float32)


def kernel(n, q_hbm, k_hbm, v_hbm, p_hbm, len_ref, of_ref, out_hbm,
           q_ref, k_ref, v_ref, own_prompts, far_prompts, out_ref, intra, first, sum_out, sum_in, st_out, st_in, pr_out, pr_in,
           over_out, over_in, index, flag, load_sem, out_sem, swap_sem, over_send, over_recv, sum_send, sum_recv, st_send, st_recv,
           pr_send, pr_recv):
    me = lax.axis_index("seq")
    half = n // 2
    side = me // half
    own = lax.rem(me, half)
    base = side * half
    partner = lax.rem(me + half, n)
    width = k_ref.shape[1]
    heads = width // DK
    rows = width // n
    pieces = DK // rows
    responses = len_ref.shape[0]

    def load(i, src, dst):
        return pltpu.make_async_copy(src, dst, load_sem.at[i])

    loads = [load(0, p_hbm, own_prompts), load(1, k_hbm, k_ref), load(2, v_hbm, v_ref), load(3, q_hbm, q_ref)]
    for copy in loads:
        copy.start()

    barrier = pltpu.get_barrier_semaphore()

    def greet(device):
        pl.semaphore_signal(barrier, inc=1, device_id={"seq": device}, device_id_type=pl.DeviceIdType.MESH)

    greet(partner)

    @pl.loop(1, half)
    def _(j):
        greet(base + lax.rem(own + j, half))

    @pl.loop(0, n)
    def _(i):
        c = 2 * base + i
        start = jnp.int32(0)
        begins = jnp.int32(0)
        which = jnp.int32(0)
        for r in range(responses):
            hit = jnp.where(start == c, 1, 0)
            begins = begins + hit
            which = which + hit * of_ref[r]
            start = start + len_ref[r]
        flag[i] = begins
        index[i] = which

    pl.semaphore_wait(barrier, half)

    def send(src, dst, send_sem, recv_sem, target):
        return pltpu.make_async_remote_copy(
            src_ref=src, dst_ref=dst, send_sem=send_sem, recv_sem=recv_sem,
            device_id={"seq": target}, device_id_type=pl.DeviceIdType.MESH)

    loads[0].wait()
    swap = send(own_prompts, far_prompts, swap_sem.at[0], swap_sem.at[1], partner)
    swap.start()

    def give_prompts(slot, prompts):
        @pl.loop(1, half + 1)
        def _(j):
            target = lax.rem(own + j, half)
            pr_out[target, slot] = prompts[index[2 * target + 1]]

            @pl.when(target != own)
            def _():
                send(pr_out.at[target, slot], pr_in.at[own, slot], pr_send, pr_recv.at[slot], base + target).start()

        pr_in[own, slot] = pr_out[own, slot]

    give_prompts(0, own_prompts)

    loads[1].wait()
    loads[2].wait()
    second_starts = flag[2 * own + 1] > 0

    @pl.loop(0, heads // 2)
    def _(i):
        pair = lax.rem(own // pieces + 1 + i, heads // 2)
        for slot in range(2):
            h = pair + lax.rem(side + slot, 2) * (heads // 2)
            cols = pl.ds(pl.multiple_of(h * DK, DK), DK)
            a = matmul(k_ref[0:SPAN, cols], v_ref[0:SPAN, cols], 0, 0)
            b = matmul(k_ref[SPAN:2 * SPAN, cols], v_ref[SPAN:2 * SPAN, cols], 0, 0)
            first[h] = a
            total = jnp.where(second_starts, b, a + b).astype(jnp.bfloat16)
            for j in range(pieces):
                sum_out[pair * pieces + j, slot] = total[j * rows:(j + 1) * rows]
        for j in range(pieces):
            owner = pair * pieces + j

            @pl.when(owner != own)
            def _():
                send(sum_out.at[owner], sum_in.at[own], sum_send, sum_recv.at[own], base + owner).start()

    sum_in[own] = sum_out[own]

    loads[3].wait()
    causal = lax.broadcasted_iota(jnp.int32, (SPAN, SPAN), 0) >= lax.broadcasted_iota(jnp.int32, (SPAN, SPAN), 1)

    def within(low, high):
        @pl.loop(low, high)
        def _(h):
            cols = pl.ds(pl.multiple_of(h * DK, DK), DK)
            for block in range(2):
                rng = slice(block * SPAN, (block + 1) * SPAN)
                scores = matmul(q_ref[rng, cols], k_ref[rng, cols], 1, 1)
                weights = jnp.where(causal, scores, 0.0).astype(jnp.bfloat16)
                intra[rng, cols] = matmul(weights, v_ref[rng, cols], 1, 0)

    within(0, heads // 2)

    @pl.loop(1, half)
    def _(j):
        d = lax.rem(own + half - j, half)
        send(sum_out.at[d], sum_in.at[d], sum_send, sum_recv.at[d], base + d).wait_recv()

    def scan(slot, prompts, state):
        def step(d, state):
            state = jnp.where(flag[2 * d] > 0, prompts[index[2 * d]].astype(jnp.float32), state)
            st_out[d, slot] = state.astype(jnp.bfloat16)
            state = jnp.where(flag[2 * d + 1] > 0, prompts[index[2 * d + 1]].astype(jnp.float32), state)
            return state + sum_in[d, slot].astype(jnp.float32)

        return lax.fori_loop(0, half, step, state)

    def give_states(slot):
        @pl.loop(1, half)
        def _(j):
            d = lax.rem(own + j, half)
            send(st_out.at[d, slot], st_in.at[own, slot], st_send, st_recv.at[slot, own], base + d).start()

        st_in[own, slot] = st_out[own, slot]

    def over(slot):
        return send(over_out.at[slot], over_in.at[1 - slot], over_send.at[slot], over_recv.at[1 - slot], partner)

    def arrived(slot):
        over(1 - slot).wait_recv()
        return over_in[slot].astype(jnp.float32)

    def hand_over(slot, state):
        over_out[slot] = state.astype(jnp.bfloat16)
        over(slot).start()

    nothing = jnp.zeros((rows, DV), jnp.float32)

    @pl.when(side == 0)
    def _():
        hand_over(0, scan(0, own_prompts, nothing))
        give_states(0)

    within(heads // 2, heads)
    swap.wait_recv()

    @pl.when(side == 0)
    def _():
        hand_over(1, scan(1, far_prompts, nothing))
        give_states(1)
        give_prompts(1, far_prompts)

    @pl.when(side == 1)
    def _():
        scan(1, far_prompts, arrived(1))
        give_states(1)
        give_prompts(1, far_prompts)
        scan(0, own_prompts, arrived(0))
        give_states(0)

    def others(ref):
        return ref.at[0:half - 1]

    @pl.loop(0, 2)
    def _(turn):
        slot = lax.rem(side + turn, 2)
        pltpu.make_async_copy(pr_in.at[0:half - 1, 0], pr_in.at[0:half - 1, 0], pr_recv.at[slot]).wait()

        @pl.loop(0, heads // 2)
        def _(i):
            pair = lax.rem(own // pieces + heads // 2 - i, heads // 2)
            for j in range(pieces):
                owner = pair * pieces + j

                @pl.when(owner != own)
                def _():
                    send(st_out.at[owner, slot], st_in.at[owner, slot], st_send, st_recv.at[slot, owner], base + owner).wait_recv()

            h = pair + lax.rem(side + slot, 2) * (heads // 2)
            cols = pl.ds(pl.multiple_of(h * DK, DK), DK)
            entering = st_in[pl.ds(pair * pieces, pieces), slot].reshape(DK, DV)
            prompt = pr_in[pl.ds(pair * pieces, pieces), slot].reshape(DK, DV)
            later = (entering.astype(jnp.float32) + first[h]).astype(jnp.bfloat16)
            states = (entering, jnp.where(second_starts, prompt, later))
            for block in range(2):
                rng = slice(block * SPAN, (block + 1) * SPAN)
                o = matmul(q_ref[rng, cols], states[block], 1, 0) + intra[rng, cols]
                scale = lax.rsqrt(jnp.mean(o * o, axis=-1, keepdims=True) + epsilon)
                out_ref[rng, cols] = (o * scale).astype(jnp.bfloat16)
            pltpu.make_async_copy(out_ref.at[:, cols], out_hbm.at[:, cols], out_sem).start()

    pltpu.make_async_copy(out_ref, out_hbm, out_sem).wait()
    swap.wait_send()
    pltpu.make_async_copy(others(pr_out), others(pr_out), pr_send).wait()
    pltpu.make_async_copy(others(sum_out), others(sum_out), sum_send).wait()
    pltpu.make_async_copy(others(st_out), others(st_out), st_send).wait()

    @pl.when(side == 0)
    def _():
        over(0).wait_send()
        over(1).wait_send()


def solution(mesh):
    n = mesh.shape["seq"]

    def shards(queries, keys, values, prompt_state, lengths, prompt_of):
        tokens, width = queries.shape
        prompts, rows, _ = prompt_state.shape
        half = jnp.bfloat16
        anywhere = pl.BlockSpec(memory_space=pl.ANY)
        scalar = pl.BlockSpec(memory_space=pltpu.SMEM)
        piece = pltpu.VMEM((n // 2, 2, rows, DV), half)
        dma = pltpu.SemaphoreType.DMA
        return pl.pallas_call(
            functools.partial(kernel, n),
            out_shape=jax.ShapeDtypeStruct((tokens, width), half),
            in_specs=[anywhere] * 4 + [scalar] * 2,
            out_specs=anywhere,
            scratch_shapes=[
                pltpu.VMEM((tokens, width), half),
                pltpu.VMEM((tokens, width), half),
                pltpu.VMEM((tokens, width), half),
                pltpu.VMEM((prompts, rows, DV), half),
                pltpu.VMEM((prompts, rows, DV), half),
                pltpu.VMEM((tokens, width), half),
                pltpu.VMEM((tokens, width), jnp.float32),
                pltpu.VMEM((width // DK, DK, DV), jnp.float32),
                piece, piece, piece, piece, piece, piece,
                pltpu.VMEM((2, rows, DV), half),
                pltpu.VMEM((2, rows, DV), half),
                pltpu.SMEM((n,), jnp.int32),
                pltpu.SMEM((n,), jnp.int32),
                dma((4,)), dma(()), dma((2,)), dma((2,)), dma((2,)),
                dma(()), dma((n // 2,)), dma(()), dma((2, n // 2)), dma(()), dma((2,)),
            ],
            compiler_params=pltpu.CompilerParams(
                collective_id=0, has_side_effects=True, vmem_limit_bytes=62 << 20),
        )(queries, keys, values, prompt_state, lengths, prompt_of.reshape(-1))

    placed = (
        P(("groups", "seq"), None),
        P(("groups", "seq"), None),
        P(("groups", "seq"), None),
        P("groups", "seq", None),
        P("groups"),
        P("groups", None),
    )
    return jax.shard_map(
        shards, mesh=mesh, in_specs=placed, out_specs=P(("groups", "seq"), None), check_vma=False
    )
```

```python
import functools
import jax
import jax.numpy as jnp
from jax import lax
from jax.experimental import pallas as pl
from jax.experimental.pallas import tpu as pltpu
from jax.sharding import PartitionSpec as P

DK = 128
DV = 128
SPAN = 128
epsilon = 1e-06


def matmul(a, b, ca, cb):
    return lax.dot_general(a, b, (((ca,), (cb,)), ((), ())), preferred_element_type=jnp.float32)


def kernel(n, q_hbm, k_hbm, v_hbm, p_hbm, len_ref, of_ref, out_hbm,
           q_ref, k_ref, v_ref, own_prompts, far_prompts, out_ref, intra, first, sum_out, sum_in, st_out, st_in, pr_out, pr_in,
           over_out, over_in, index, flag, load_sem, out_sem, swap_sem, over_send, over_recv, sum_send, sum_recv, st_send, st_recv,
           pr_send, pr_recv):
    me = lax.axis_index("seq")
    half = n // 2
    side = me // half
    own = lax.rem(me, half)
    base = side * half
    partner = lax.rem(me + half, n)
    width = k_ref.shape[1]
    heads = width // DK
    rows = width // n
    pieces = DK // rows
    responses = len_ref.shape[0]

    def load(i, src, dst):
        return pltpu.make_async_copy(src, dst, load_sem.at[i])

    loads = [load(0, p_hbm, own_prompts), load(1, k_hbm, k_ref), load(2, v_hbm, v_ref), load(3, q_hbm, q_ref)]
    for copy in loads:
        copy.start()

    barrier = pltpu.get_barrier_semaphore()

    def greet(device):
        pl.semaphore_signal(barrier, inc=1, device_id={"seq": device}, device_id_type=pl.DeviceIdType.MESH)

    greet(partner)

    @pl.loop(1, half)
    def _(j):
        greet(base + lax.rem(own + j, half))

    @pl.loop(0, n)
    def _(i):
        c = 2 * base + i
        start = jnp.int32(0)
        begins = jnp.int32(0)
        which = jnp.int32(0)
        for r in range(responses):
            hit = jnp.where(start == c, 1, 0)
            begins = begins + hit
            which = which + hit * of_ref[r]
            start = start + len_ref[r]
        flag[i] = begins
        index[i] = which

    pl.semaphore_wait(barrier, half)

    def send(src, dst, send_sem, recv_sem, target):
        return pltpu.make_async_remote_copy(
            src_ref=src, dst_ref=dst, send_sem=send_sem, recv_sem=recv_sem,
            device_id={"seq": target}, device_id_type=pl.DeviceIdType.MESH)

    loads[0].wait()
    swap = send(own_prompts, far_prompts, swap_sem.at[0], swap_sem.at[1], partner)
    swap.start()

    def give_prompts(slot, prompts):
        @pl.loop(1, half + 1)
        def _(j):
            target = lax.rem(own + j, half)
            pr_out[target, slot] = prompts[index[2 * target + 1]]

            @pl.when(target != own)
            def _():
                send(pr_out.at[target, slot], pr_in.at[own, slot], pr_send, pr_recv.at[slot], base + target).start()

        pr_in[own, slot] = pr_out[own, slot]

    loads[1].wait()
    loads[2].wait()
    second_starts = flag[2 * own + 1] > 0

    @pl.loop(0, heads // 2)
    def _(i):
        pair = lax.rem(own // pieces + 1 + i, heads // 2)
        for slot in range(2):
            h = pair + lax.rem(side + slot, 2) * (heads // 2)
            cols = pl.ds(pl.multiple_of(h * DK, DK), DK)
            a = matmul(k_ref[0:SPAN, cols], v_ref[0:SPAN, cols], 0, 0)
            b = matmul(k_ref[SPAN:2 * SPAN, cols], v_ref[SPAN:2 * SPAN, cols], 0, 0)
            first[h] = a
            total = jnp.where(second_starts, b, a + b).astype(jnp.bfloat16)
            for j in range(pieces):
                sum_out[pair * pieces + j, slot] = total[j * rows:(j + 1) * rows]
        for j in range(pieces):
            owner = pair * pieces + j

            @pl.when(owner != own)
            def _():
                send(sum_out.at[owner], sum_in.at[own], sum_send, sum_recv.at[own], base + owner).start()

    sum_in[own] = sum_out[own]

    loads[3].wait()
    causal = lax.broadcasted_iota(jnp.int32, (SPAN, SPAN), 0) >= lax.broadcasted_iota(jnp.int32, (SPAN, SPAN), 1)

    def within(low, high):
        @pl.loop(low, high)
        def _(h):
            cols = pl.ds(pl.multiple_of(h * DK, DK), DK)
            for block in range(2):
                rng = slice(block * SPAN, (block + 1) * SPAN)
                scores = matmul(q_ref[rng, cols], k_ref[rng, cols], 1, 1)
                weights = jnp.where(causal, scores, 0.0).astype(jnp.bfloat16)
                intra[rng, cols] = matmul(weights, v_ref[rng, cols], 1, 0)

    def sums_arrived():
        @pl.loop(1, half)
        def _(j):
            d = lax.rem(own + half - j, half)
            send(sum_out.at[d], sum_in.at[d], sum_send, sum_recv.at[d], base + d).wait_recv()

    def scan(slot, prompts, state):
        def step(d, state):
            state = jnp.where(flag[2 * d] > 0, prompts[index[2 * d]].astype(jnp.float32), state)
            st_out[d, slot] = state.astype(jnp.bfloat16)
            state = jnp.where(flag[2 * d + 1] > 0, prompts[index[2 * d + 1]].astype(jnp.float32), state)
            return state + sum_in[d, slot].astype(jnp.float32)

        return lax.fori_loop(0, half, step, state)

    def give_states(slot):
        @pl.loop(1, half)
        def _(j):
            d = lax.rem(own + j, half)
            send(st_out.at[d, slot], st_in.at[own, slot], st_send, st_recv.at[slot, own], base + d).start()

        st_in[own, slot] = st_out[own, slot]

    def over(slot):
        return send(over_out.at[slot], over_in.at[1 - slot], over_send.at[slot], over_recv.at[1 - slot], partner)

    def arrived(slot):
        over(1 - slot).wait_recv()
        return over_in[slot].astype(jnp.float32)

    def hand_over(slot, state):
        over_out[slot] = state.astype(jnp.bfloat16)
        over(slot).start()

    nothing = jnp.zeros((rows, DV), jnp.float32)

    give_prompts(0, own_prompts)
    within(0, heads)
    sums_arrived()

    @pl.when(side == 0)
    def _():
        hand_over(0, scan(0, own_prompts, nothing))
        give_states(0)
        swap.wait_recv()
        hand_over(1, scan(1, far_prompts, nothing))
        give_states(1)
        give_prompts(1, far_prompts)

    @pl.when(side == 1)
    def _():
        swap.wait_recv()
        give_prompts(1, far_prompts)
        scan(1, far_prompts, arrived(1))
        give_states(1)
        scan(0, own_prompts, arrived(0))
        give_states(0)

    def others(ref):
        return ref.at[0:half - 1]

    @pl.loop(0, 2)
    def _(turn):
        slot = lax.rem(side + turn, 2)
        pltpu.make_async_copy(pr_in.at[0:half - 1, 0], pr_in.at[0:half - 1, 0], pr_recv.at[slot]).wait()

        @pl.loop(0, heads // 2)
        def _(i):
            pair = lax.rem(own // pieces + heads // 2 - i, heads // 2)
            for j in range(pieces):
                owner = pair * pieces + j

                @pl.when(owner != own)
                def _():
                    send(st_out.at[owner, slot], st_in.at[owner, slot], st_send, st_recv.at[slot, owner], base + owner).wait_recv()

            h = pair + lax.rem(side + slot, 2) * (heads // 2)
            cols = pl.ds(pl.multiple_of(h * DK, DK), DK)
            entering = st_in[pl.ds(pair * pieces, pieces), slot].reshape(DK, DV)
            prompt = pr_in[pl.ds(pair * pieces, pieces), slot].reshape(DK, DV)
            later = (entering.astype(jnp.float32) + first[h]).astype(jnp.bfloat16)
            states = (entering, jnp.where(second_starts, prompt, later))
            for block in range(2):
                rng = slice(block * SPAN, (block + 1) * SPAN)
                o = matmul(q_ref[rng, cols], states[block], 1, 0) + intra[rng, cols]
                scale = lax.rsqrt(jnp.mean(o * o, axis=-1, keepdims=True) + epsilon)
                out_ref[rng, cols] = (o * scale).astype(jnp.bfloat16)
            pltpu.make_async_copy(out_ref.at[:, cols], out_hbm.at[:, cols], out_sem).start()

    pltpu.make_async_copy(out_ref, out_hbm, out_sem).wait()
    swap.wait_send()
    pltpu.make_async_copy(others(pr_out), others(pr_out), pr_send).wait()
    pltpu.make_async_copy(others(sum_out), others(sum_out), sum_send).wait()
    pltpu.make_async_copy(others(st_out), others(st_out), st_send).wait()

    @pl.when(side == 0)
    def _():
        over(0).wait_send()
        over(1).wait_send()


def solution(mesh):
    n = mesh.shape["seq"]

    def shards(queries, keys, values, prompt_state, lengths, prompt_of):
        tokens, width = queries.shape
        prompts, rows, _ = prompt_state.shape
        half = jnp.bfloat16
        anywhere = pl.BlockSpec(memory_space=pl.ANY)
        scalar = pl.BlockSpec(memory_space=pltpu.SMEM)
        piece = pltpu.VMEM((n // 2, 2, rows, DV), half)
        dma = pltpu.SemaphoreType.DMA
        return pl.pallas_call(
            functools.partial(kernel, n),
            out_shape=jax.ShapeDtypeStruct((tokens, width), half),
            in_specs=[anywhere] * 4 + [scalar] * 2,
            out_specs=anywhere,
            scratch_shapes=[
                pltpu.VMEM((tokens, width), half),
                pltpu.VMEM((tokens, width), half),
                pltpu.VMEM((tokens, width), half),
                pltpu.VMEM((prompts, rows, DV), half),
                pltpu.VMEM((prompts, rows, DV), half),
                pltpu.VMEM((tokens, width), half),
                pltpu.VMEM((tokens, width), jnp.float32),
                pltpu.VMEM((width // DK, DK, DV), jnp.float32),
                piece, piece, piece, piece, piece, piece,
                pltpu.VMEM((2, rows, DV), half),
                pltpu.VMEM((2, rows, DV), half),
                pltpu.SMEM((n,), jnp.int32),
                pltpu.SMEM((n,), jnp.int32),
                dma((4,)), dma(()), dma((2,)), dma((2,)), dma((2,)),
                dma(()), dma((n // 2,)), dma(()), dma((2, n // 2)), dma(()), dma((2,)),
            ],
            compiler_params=pltpu.CompilerParams(
                collective_id=0, has_side_effects=True, vmem_limit_bytes=62 << 20),
        )(queries, keys, values, prompt_state, lengths, prompt_of.reshape(-1))

    placed = (
        P(("groups", "seq"), None),
        P(("groups", "seq"), None),
        P(("groups", "seq"), None),
        P("groups", "seq", None),
        P("groups"),
        P("groups", None),
    )
    return jax.shard_map(
        shards, mesh=mesh, in_specs=placed, out_specs=P(("groups", "seq"), None), check_vma=False
    )
```

```python
import functools
import jax
import jax.numpy as jnp
from jax import lax
from jax.experimental import pallas as pl
from jax.experimental.pallas import tpu as pltpu
from jax.sharding import PartitionSpec as P

DK = 128
DV = 128
SPAN = 128
epsilon = 1e-06


def matmul(a, b, ca, cb):
    return lax.dot_general(a, b, (((ca,), (cb,)), ((), ())), preferred_element_type=jnp.float32)


def kernel(n, q_hbm, k_hbm, v_hbm, p_hbm, len_ref, of_ref, out_hbm,
           q_ref, k_ref, v_ref, own_prompts, far_prompts, out_ref, intra, first, sum_out, sum_in, st_out, st_in, pr_out, pr_in,
           over_out, over_in, index, flag, load_sem, out_sem, swap_sem, over_send, over_recv, sum_send, sum_recv, st_send, st_recv,
           pr_send, pr_recv):
    me = lax.axis_index("seq")
    half = n // 2
    side = me // half
    own = lax.rem(me, half)
    base = side * half
    partner = lax.rem(me + half, n)
    width = k_ref.shape[1]
    heads = width // DK
    rows = width // n
    pieces = DK // rows
    responses = len_ref.shape[0]

    def load(i, src, dst):
        return pltpu.make_async_copy(src, dst, load_sem.at[i])

    loads = [load(0, p_hbm, own_prompts), load(1, k_hbm, k_ref), load(2, v_hbm, v_ref), load(3, q_hbm, q_ref)]
    for copy in loads:
        copy.start()

    barrier = pltpu.get_barrier_semaphore()

    def greet(device):
        pl.semaphore_signal(barrier, inc=1, device_id={"seq": device}, device_id_type=pl.DeviceIdType.MESH)

    greet(partner)

    @pl.loop(1, half)
    def _(j):
        greet(base + lax.rem(own + j, half))

    @pl.loop(0, n)
    def _(i):
        c = 2 * base + i
        start = jnp.int32(0)
        begins = jnp.int32(0)
        which = jnp.int32(0)
        for r in range(responses):
            hit = jnp.where(start == c, 1, 0)
            begins = begins + hit
            which = which + hit * of_ref[r]
            start = start + len_ref[r]
        flag[i] = begins
        index[i] = which

    pl.semaphore_wait(barrier, half)

    def send(src, dst, send_sem, recv_sem, target):
        return pltpu.make_async_remote_copy(
            src_ref=src, dst_ref=dst, send_sem=send_sem, recv_sem=recv_sem,
            device_id={"seq": target}, device_id_type=pl.DeviceIdType.MESH)

    loads[0].wait()
    swap = send(own_prompts, far_prompts, swap_sem.at[0], swap_sem.at[1], partner)
    swap.start()

    def give_prompts(slot, prompts):
        @pl.loop(1, half + 1)
        def _(j):
            target = lax.rem(own + j, half)
            pr_out[target, slot] = prompts[index[2 * target + 1]]

            @pl.when(target != own)
            def _():
                send(pr_out.at[target, slot], pr_in.at[own, slot], pr_send, pr_recv.at[slot], base + target).start()

        pr_in[own, slot] = pr_out[own, slot]

    loads[1].wait()
    loads[2].wait()
    second_starts = flag[2 * own + 1] > 0

    @pl.loop(0, heads // 2)
    def _(i):
        pair = lax.rem(own // pieces + 1 + i, heads // 2)
        for slot in range(2):
            h = pair + lax.rem(side + slot, 2) * (heads // 2)
            cols = pl.ds(pl.multiple_of(h * DK, DK), DK)
            a = matmul(k_ref[0:SPAN, cols], v_ref[0:SPAN, cols], 0, 0)
            b = matmul(k_ref[SPAN:2 * SPAN, cols], v_ref[SPAN:2 * SPAN, cols], 0, 0)
            first[h] = a
            total = jnp.where(second_starts, b, a + b).astype(jnp.bfloat16)
            for j in range(pieces):
                sum_out[pair * pieces + j, slot] = total[j * rows:(j + 1) * rows]
        for j in range(pieces):
            owner = pair * pieces + j

            @pl.when(owner != own)
            def _():
                send(sum_out.at[owner], sum_in.at[own], sum_send, sum_recv.at[own], base + owner).start()

    sum_in[own] = sum_out[own]

    loads[3].wait()
    causal = lax.broadcasted_iota(jnp.int32, (SPAN, SPAN), 0) >= lax.broadcasted_iota(jnp.int32, (SPAN, SPAN), 1)

    def within(low, high):
        @pl.loop(low, high)
        def _(h):
            cols = pl.ds(pl.multiple_of(h * DK, DK), DK)
            for block in range(2):
                rng = slice(block * SPAN, (block + 1) * SPAN)
                scores = matmul(q_ref[rng, cols], k_ref[rng, cols], 1, 1)
                weights = jnp.where(causal, scores, 0.0).astype(jnp.bfloat16)
                intra[rng, cols] = matmul(weights, v_ref[rng, cols], 1, 0)

    def sums_arrived():
        @pl.loop(1, half)
        def _(j):
            d = lax.rem(own + half - j, half)
            send(sum_out.at[d], sum_in.at[d], sum_send, sum_recv.at[d], base + d).wait_recv()

    def scan(slot, prompts, state):
        def step(d, state):
            state = jnp.where(flag[2 * d] > 0, prompts[index[2 * d]].astype(jnp.float32), state)
            st_out[d, slot] = state.astype(jnp.bfloat16)
            state = jnp.where(flag[2 * d + 1] > 0, prompts[index[2 * d + 1]].astype(jnp.float32), state)
            return state + sum_in[d, slot].astype(jnp.float32)

        return lax.fori_loop(0, half, step, state)

    def give_states(slot):
        @pl.loop(1, half)
        def _(j):
            d = lax.rem(own + j, half)
            send(st_out.at[d, slot], st_in.at[own, slot], st_send, st_recv.at[slot, own], base + d).start()

        st_in[own, slot] = st_out[own, slot]

    def over(slot):
        return send(over_out.at[slot], over_in.at[1 - slot], over_send.at[slot], over_recv.at[1 - slot], partner)

    def arrived(slot):
        over(1 - slot).wait_recv()
        return over_in[slot].astype(jnp.float32)

    def hand_over(slot, state):
        over_out[slot] = state.astype(jnp.bfloat16)
        over(slot).start()

    nothing = jnp.zeros((rows, DV), jnp.float32)

    give_prompts(0, own_prompts)
    within(0, heads)
    sums_arrived()

    @pl.when(side == 0)
    def _():
        hand_over(0, scan(0, own_prompts, nothing))
        give_states(0)
        swap.wait_recv()
        hand_over(1, scan(1, far_prompts, nothing))
        give_prompts(1, far_prompts)
        give_states(1)

    @pl.when(side == 1)
    def _():
        swap.wait_recv()
        give_prompts(1, far_prompts)
        scan(1, far_prompts, arrived(1))
        give_states(1)
        scan(0, own_prompts, arrived(0))
        give_states(0)

    def others(ref):
        return ref.at[0:half - 1]

    @pl.loop(0, 2)
    def _(turn):
        slot = lax.rem(side + turn, 2)
        pltpu.make_async_copy(pr_in.at[0:half - 1, 0], pr_in.at[0:half - 1, 0], pr_recv.at[slot]).wait()

        @pl.loop(0, heads // 2)
        def _(i):
            pair = lax.rem(own // pieces + heads // 2 - i, heads // 2)
            for j in range(pieces):
                owner = pair * pieces + j

                @pl.when(owner != own)
                def _():
                    send(st_out.at[owner, slot], st_in.at[owner, slot], st_send, st_recv.at[slot, owner], base + owner).wait_recv()

            h = pair + lax.rem(side + slot, 2) * (heads // 2)
            cols = pl.ds(pl.multiple_of(h * DK, DK), DK)
            entering = st_in[pl.ds(pair * pieces, pieces), slot].reshape(DK, DV)
            prompt = pr_in[pl.ds(pair * pieces, pieces), slot].reshape(DK, DV)
            later = (entering.astype(jnp.float32) + first[h]).astype(jnp.bfloat16)
            states = (entering, jnp.where(second_starts, prompt, later))
            for block in range(2):
                rng = slice(block * SPAN, (block + 1) * SPAN)
                o = matmul(q_ref[rng, cols], states[block], 1, 0) + intra[rng, cols]
                scale = lax.rsqrt(jnp.mean(o * o, axis=-1, keepdims=True) + epsilon)
                out_ref[rng, cols] = (o * scale).astype(jnp.bfloat16)
            pltpu.make_async_copy(out_ref.at[:, cols], out_hbm.at[:, cols], out_sem).start()

    pltpu.make_async_copy(out_ref, out_hbm, out_sem).wait()
    swap.wait_send()
    pltpu.make_async_copy(others(pr_out), others(pr_out), pr_send).wait()
    pltpu.make_async_copy(others(sum_out), others(sum_out), sum_send).wait()
    pltpu.make_async_copy(others(st_out), others(st_out), st_send).wait()

    @pl.when(side == 0)
    def _():
        over(0).wait_send()
        over(1).wait_send()


def solution(mesh):
    n = mesh.shape["seq"]

    def shards(queries, keys, values, prompt_state, lengths, prompt_of):
        tokens, width = queries.shape
        prompts, rows, _ = prompt_state.shape
        half = jnp.bfloat16
        anywhere = pl.BlockSpec(memory_space=pl.ANY)
        scalar = pl.BlockSpec(memory_space=pltpu.SMEM)
        piece = pltpu.VMEM((n // 2, 2, rows, DV), half)
        dma = pltpu.SemaphoreType.DMA
        return pl.pallas_call(
            functools.partial(kernel, n),
            out_shape=jax.ShapeDtypeStruct((tokens, width), half),
            in_specs=[anywhere] * 4 + [scalar] * 2,
            out_specs=anywhere,
            scratch_shapes=[
                pltpu.VMEM((tokens, width), half),
                pltpu.VMEM((tokens, width), half),
                pltpu.VMEM((tokens, width), half),
                pltpu.VMEM((prompts, rows, DV), half),
                pltpu.VMEM((prompts, rows, DV), half),
                pltpu.VMEM((tokens, width), half),
                pltpu.VMEM((tokens, width), jnp.float32),
                pltpu.VMEM((width // DK, DK, DV), jnp.float32),
                piece, piece, piece, piece, piece, piece,
                pltpu.VMEM((2, rows, DV), half),
                pltpu.VMEM((2, rows, DV), half),
                pltpu.SMEM((n,), jnp.int32),
                pltpu.SMEM((n,), jnp.int32),
                dma((4,)), dma(()), dma((2,)), dma((2,)), dma((2,)),
                dma(()), dma((n // 2,)), dma(()), dma((2, n // 2)), dma(()), dma((2,)),
            ],
            compiler_params=pltpu.CompilerParams(
                collective_id=0, has_side_effects=True, vmem_limit_bytes=62 << 20),
        )(queries, keys, values, prompt_state, lengths, prompt_of.reshape(-1))

    placed = (
        P(("groups", "seq"), None),
        P(("groups", "seq"), None),
        P(("groups", "seq"), None),
        P("groups", "seq", None),
        P("groups"),
        P("groups", None),
    )
    return jax.shard_map(
        shards, mesh=mesh, in_specs=placed, out_specs=P(("groups", "seq"), None), check_vma=False
    )
```

```python
import functools
import jax
import jax.numpy as jnp
from jax import lax
from jax.experimental import pallas as pl
from jax.experimental.pallas import tpu as pltpu
from jax.sharding import PartitionSpec as P

DK = 128
DV = 128
SPAN = 128
epsilon = 1e-06


def matmul(a, b, ca, cb):
    return lax.dot_general(a, b, (((ca,), (cb,)), ((), ())), preferred_element_type=jnp.float32)


def kernel(n, q_hbm, k_hbm, v_hbm, p_hbm, len_ref, of_ref, out_hbm,
           q_ref, k_ref, v_ref, own_prompts, far_prompts, out_ref, intra, first, sum_out, sum_in, st_out, st_in, pr_out, pr_in,
           over_out, over_in, index, flag, load_sem, out_sem, swap_sem, over_send, over_recv, sum_send, sum_recv, st_send, st_recv,
           pr_send, pr_recv):
    me = lax.axis_index("seq")
    half = n // 2
    side = me // half
    own = lax.rem(me, half)
    base = side * half
    partner = lax.rem(me + half, n)
    width = k_ref.shape[1]
    heads = width // DK
    rows = width // n
    pieces = DK // rows
    responses = len_ref.shape[0]

    def load(i, src, dst):
        return pltpu.make_async_copy(src, dst, load_sem.at[i])

    loads = [load(0, p_hbm, own_prompts), load(1, k_hbm, k_ref), load(2, v_hbm, v_ref), load(3, q_hbm, q_ref)]
    for copy in loads:
        copy.start()

    barrier = pltpu.get_barrier_semaphore()

    def greet(device):
        pl.semaphore_signal(barrier, inc=1, device_id={"seq": device}, device_id_type=pl.DeviceIdType.MESH)

    greet(partner)

    @pl.loop(1, half)
    def _(j):
        greet(base + lax.rem(own + j, half))

    @pl.loop(0, n)
    def _(i):
        c = 2 * base + i
        start = jnp.int32(0)
        begins = jnp.int32(0)
        which = jnp.int32(0)
        for r in range(responses):
            hit = jnp.where(start == c, 1, 0)
            begins = begins + hit
            which = which + hit * of_ref[r]
            start = start + len_ref[r]
        flag[i] = begins
        index[i] = which

    pl.semaphore_wait(barrier, half)

    def send(src, dst, send_sem, recv_sem, target):
        return pltpu.make_async_remote_copy(
            src_ref=src, dst_ref=dst, send_sem=send_sem, recv_sem=recv_sem,
            device_id={"seq": target}, device_id_type=pl.DeviceIdType.MESH)

    loads[0].wait()
    swap = send(own_prompts, far_prompts, swap_sem.at[0], swap_sem.at[1], partner)
    swap.start()

    def give_prompts(slot, prompts):
        @pl.loop(1, half + 1)
        def _(j):
            target = lax.rem(own + j, half)
            pr_out[target, slot] = prompts[index[2 * target + 1]]

            @pl.when(target != own)
            def _():
                send(pr_out.at[target, slot], pr_in.at[own, slot], pr_send, pr_recv.at[slot], base + target).start()

        pr_in[own, slot] = pr_out[own, slot]

    loads[1].wait()
    loads[2].wait()
    second_starts = flag[2 * own + 1] > 0

    @pl.loop(0, heads // 2)
    def _(i):
        pair = lax.rem(own // pieces + 1 + i, heads // 2)
        for slot in range(2):
            h = pair + lax.rem(side + slot, 2) * (heads // 2)
            cols = pl.ds(pl.multiple_of(h * DK, DK), DK)
            a = matmul(k_ref[0:SPAN, cols], v_ref[0:SPAN, cols], 0, 0)
            b = matmul(k_ref[SPAN:2 * SPAN, cols], v_ref[SPAN:2 * SPAN, cols], 0, 0)
            first[h] = a
            total = jnp.where(second_starts, b, a + b).astype(jnp.bfloat16)
            for j in range(pieces):
                sum_out[pair * pieces + j, slot] = total[j * rows:(j + 1) * rows]
        for j in range(pieces):
            owner = pair * pieces + j

            @pl.when(owner != own)
            def _():
                send(sum_out.at[owner], sum_in.at[own], sum_send, sum_recv.at[own], base + owner).start()

    sum_in[own] = sum_out[own]

    loads[3].wait()
    causal = lax.broadcasted_iota(jnp.int32, (SPAN, SPAN), 0) >= lax.broadcasted_iota(jnp.int32, (SPAN, SPAN), 1)

    def within(low, high):
        @pl.loop(low, high)
        def _(h):
            cols = pl.ds(pl.multiple_of(h * DK, DK), DK)
            for block in range(2):
                rng = slice(block * SPAN, (block + 1) * SPAN)
                scores = matmul(q_ref[rng, cols], k_ref[rng, cols], 1, 1)
                weights = jnp.where(causal, scores, 0.0).astype(jnp.bfloat16)
                intra[rng, cols] = matmul(weights, v_ref[rng, cols], 1, 0)

    def sums_arrived():
        @pl.loop(1, half)
        def _(j):
            d = lax.rem(own + half - j, half)
            send(sum_out.at[d], sum_in.at[d], sum_send, sum_recv.at[d], base + d).wait_recv()

    def scan(slot, prompts, state):
        def step(d, state):
            state = jnp.where(flag[2 * d] > 0, prompts[index[2 * d]].astype(jnp.float32), state)
            st_out[d, slot] = state.astype(jnp.bfloat16)
            state = jnp.where(flag[2 * d + 1] > 0, prompts[index[2 * d + 1]].astype(jnp.float32), state)
            return state + sum_in[d, slot].astype(jnp.float32)

        return lax.fori_loop(0, half, step, state)

    def give_states(slot):
        @pl.loop(1, half)
        def _(j):
            d = lax.rem(own + j, half)
            send(st_out.at[d, slot], st_in.at[own, slot], st_send, st_recv.at[slot, own], base + d).start()

        st_in[own, slot] = st_out[own, slot]

    def over(slot):
        return send(over_out.at[slot], over_in.at[1 - slot], over_send.at[slot], over_recv.at[1 - slot], partner)

    def arrived(slot):
        over(1 - slot).wait_recv()
        return over_in[slot].astype(jnp.float32)

    def hand_over(slot, state):
        over_out[slot] = state.astype(jnp.bfloat16)
        over(slot).start()

    nothing = jnp.zeros((rows, DV), jnp.float32)

    give_prompts(0, own_prompts)
    within(0, heads)
    sums_arrived()

    @pl.when(side == 0)
    def _():
        hand_over(0, scan(0, own_prompts, nothing))
        give_states(0)
        swap.wait_recv()
        give_prompts(1, far_prompts)
        hand_over(1, scan(1, far_prompts, nothing))
        give_states(1)

    @pl.when(side == 1)
    def _():
        swap.wait_recv()
        give_prompts(1, far_prompts)
        scan(1, far_prompts, arrived(1))
        give_states(1)
        scan(0, own_prompts, arrived(0))
        give_states(0)

    def others(ref):
        return ref.at[0:half - 1]

    @pl.loop(0, 2)
    def _(turn):
        slot = lax.rem(side + turn, 2)
        pltpu.make_async_copy(pr_in.at[0:half - 1, 0], pr_in.at[0:half - 1, 0], pr_recv.at[slot]).wait()

        @pl.loop(0, heads // 2)
        def _(i):
            pair = lax.rem(own // pieces + heads // 2 - i, heads // 2)
            for j in range(pieces):
                owner = pair * pieces + j

                @pl.when(owner != own)
                def _():
                    send(st_out.at[owner, slot], st_in.at[owner, slot], st_send, st_recv.at[slot, owner], base + owner).wait_recv()

            h = pair + lax.rem(side + slot, 2) * (heads // 2)
            cols = pl.ds(pl.multiple_of(h * DK, DK), DK)
            entering = st_in[pl.ds(pair * pieces, pieces), slot].reshape(DK, DV)
            prompt = pr_in[pl.ds(pair * pieces, pieces), slot].reshape(DK, DV)
            later = (entering.astype(jnp.float32) + first[h]).astype(jnp.bfloat16)
            states = (entering, jnp.where(second_starts, prompt, later))
            for block in range(2):
                rng = slice(block * SPAN, (block + 1) * SPAN)
                o = matmul(q_ref[rng, cols], states[block], 1, 0) + intra[rng, cols]
                scale = lax.rsqrt(jnp.mean(o * o, axis=-1, keepdims=True) + epsilon)
                out_ref[rng, cols] = (o * scale).astype(jnp.bfloat16)
            pltpu.make_async_copy(out_ref.at[:, cols], out_hbm.at[:, cols], out_sem).start()

    pltpu.make_async_copy(out_ref, out_hbm, out_sem).wait()
    swap.wait_send()
    pltpu.make_async_copy(others(pr_out), others(pr_out), pr_send).wait()
    pltpu.make_async_copy(others(sum_out), others(sum_out), sum_send).wait()
    pltpu.make_async_copy(others(st_out), others(st_out), st_send).wait()

    @pl.when(side == 0)
    def _():
        over(0).wait_send()
        over(1).wait_send()


def solution(mesh):
    n = mesh.shape["seq"]

    def shards(queries, keys, values, prompt_state, lengths, prompt_of):
        tokens, width = queries.shape
        prompts, rows, _ = prompt_state.shape
        half = jnp.bfloat16
        anywhere = pl.BlockSpec(memory_space=pl.ANY)
        scalar = pl.BlockSpec(memory_space=pltpu.SMEM)
        piece = pltpu.VMEM((n // 2, 2, rows, DV), half)
        dma = pltpu.SemaphoreType.DMA
        return pl.pallas_call(
            functools.partial(kernel, n),
            out_shape=jax.ShapeDtypeStruct((tokens, width), half),
            in_specs=[anywhere] * 4 + [scalar] * 2,
            out_specs=anywhere,
            scratch_shapes=[
                pltpu.VMEM((tokens, width), half),
                pltpu.VMEM((tokens, width), half),
                pltpu.VMEM((tokens, width), half),
                pltpu.VMEM((prompts, rows, DV), half),
                pltpu.VMEM((prompts, rows, DV), half),
                pltpu.VMEM((tokens, width), half),
                pltpu.VMEM((tokens, width), jnp.float32),
                pltpu.VMEM((width // DK, DK, DV), jnp.float32),
                piece, piece, piece, piece, piece, piece,
                pltpu.VMEM((2, rows, DV), half),
                pltpu.VMEM((2, rows, DV), half),
                pltpu.SMEM((n,), jnp.int32),
                pltpu.SMEM((n,), jnp.int32),
                dma((4,)), dma(()), dma((2,)), dma((2,)), dma((2,)),
                dma(()), dma((n // 2,)), dma(()), dma((2, n // 2)), dma(()), dma((2,)),
            ],
            compiler_params=pltpu.CompilerParams(
                collective_id=0, has_side_effects=True, vmem_limit_bytes=62 << 20),
        )(queries, keys, values, prompt_state, lengths, prompt_of.reshape(-1))

    placed = (
        P(("groups", "seq"), None),
        P(("groups", "seq"), None),
        P(("groups", "seq"), None),
        P("groups", "seq", None),
        P("groups"),
        P("groups", None),
    )
    return jax.shard_map(
        shards, mesh=mesh, in_specs=placed, out_specs=P(("groups", "seq"), None), check_vma=False
    )
```
